256 devices in a mesh: walker: 16 (over z, core), col: 16 (over y, x).
Axes of the slice: x: 4, y: 4, z: 8, core: 2. Of those that a mesh axis runs over, the one named last changes fastest.
Arguments:
- inverses: float32 [16, 4096, 4096], P('walker', None, 'col'), may hold values from -0.2 to 2.2
- table: bfloat16 [512, 64, 4096], P('walker', None, 'col'), may hold values from -0.23925781 to 0.23925781
- spots: float32 [3, 6, 16, 64], P(None, None, 'walker'), may hold values from 0 to 1
- groups: int32 [6, 16, 64, 1], P(None, 'walker'), may hold values from 0 to 15; in each aligned block of 64 rows (0 to 63, 64 to 127, ..., all dimensions but the last counted through in order) at most 8 rows name the same one
- bricks: int32 [6, 16, 64], P(None, 'walker'), may hold values from 0 to 31
- accept: int32 [6, 16, 64], P(None, 'walker'), may hold values 0 or 1
- movers: int32 [6, 16, 64], P(None, 'walker'), may hold values from 0 to 4095, as said below
- old_rows: bfloat16 [6, 16, 64, 4096], P(None, 'walker', None, 'col'), may hold values from -0.079589844 to 0.079589844
Outputs:
- updated: float32 [16, 4096, 4096], P('walker', None, 'col')
The draws below stay inside these ranges and needn't reach their ends.
Inputs may be any that keep to these rules, and one draw needn't show every extreme that they name: `groups`: in each window, at most 8 of one walker's 64 moves name one server group, and in some windows and walkers exactly 8 do. `movers`: the 64 electrons of one window and walker are distinct.
All inputs are finite; a program needn't handle non-finite values. No bound on the sum of `accept` on one device may be relied on, other than what follows from the above.
Results may differ from the reference program's by a relative error of at most 0.005.
Values may be sent and summed in bfloat16 or wider, within the bound.
No kernel may reach another device: no remote copies, remote signals or barrier semaphores. Data moves between devices by JAX's collectives and lax.ppermute only.
A program may use at most 128 MiB of HBM per device.

```python
import math
import jax
import jax.numpy as jnp
import numpy as np
from jax import lax

N = 4096
K = 64
P_SIZE = 64
NEWTON = 3
CAP = 8
ROUNDS = 6
REG_DEV = 32
WALKERS = 16
BRICKS = 512


def draw_inverses(key, part):
    first, second = jax.random.split(jax.random.fold_in(key, 11))
    spread = 0.64 / math.sqrt(N) * jax.random.normal(first, (WALKERS, N, N), jnp.float32)
    spread = jnp.clip(spread, -0.2, 0.2)
    diagonal = jax.random.uniform(second, (WALKERS, N, 1), jnp.float32, 1.0, 2.0)
    row_index = jnp.arange(N, dtype=jnp.int32)[:, None]
    col_index = jnp.arange(N, dtype=jnp.int32)[None, :]
    return jnp.where((row_index == col_index)[None], diagonal, spread)


def draw_movers(key, part):
    keys = jax.random.split(jax.random.fold_in(key, 23), ROUNDS * WALKERS)

    def choose_row(one_key):
        return jax.random.permutation(one_key, N)[:K]
    return jax.vmap(choose_row)(keys).reshape(ROUNDS, WALKERS, K).astype(jnp.int32)


def with_ends(array, key, low, top_value):
    longest = array.shape.index(max(array.shape))
    spots = []
    for shift in (0, 1):
        where = [jax.random.randint(jax.random.fold_in(key, axis), (), 0, length) for axis, length in enumerate(array.shape)]
        where[longest] = (where[longest] + shift) % array.shape[longest]
        spots.append(tuple(where))
    return array.at[spots[0]].set(low).at[spots[1]].set(top_value)


def block_scale(key, extent, cuts, smallest, largest):
    def one(axis_at, parts):
        steps = jax.random.uniform(jax.random.fold_in(jax.random.fold_in(key, 6), axis_at), (parts,), jnp.float32, smallest / len(cuts), largest / len(cuts))
        return jnp.repeat(jnp.exp(steps), extent[axis_at] // parts).reshape((-1,) + (1,) * (len(extent) - axis_at - 1))

    gain = one(*cuts[0])
    for cut in cuts[1:]:
        gain = gain * one(*cut)
    return gain


def shared_out(stream_key, own, number, rows, amount, top, most, slope):
    ranking = jax.random.permutation(stream_key, amount)
    crowded, ordinary = shares(amount, rows * top, most, slope, True), shares(amount, rows * top, most, slope, False)
    places = jnp.arange(amount)

    def named(lengths, turn):
        used = int((lengths > 0).sum())
        fixed = max(1, used // 4)
        shifted = fixed + (places - fixed + turn * (used - fixed)) % max(1, amount - fixed)
        return jnp.zeros((amount,), jnp.int32).at[ranking[jnp.where(places < fixed, places, shifted)]].set(jnp.asarray(lengths, jnp.int32))

    lengths = jnp.where(number % 4 == 0, named(crowded, number // 4), named(ordinary, number - number // 4 - 1))
    mixed = jax.random.permutation(jax.random.fold_in(own, 3), amount)
    source_of, sink = mixed[0:amount // 2 * 2:2], mixed[1:amount // 2 * 2:2]
    margin = jnp.minimum(lengths[source_of] - 1, most - lengths[sink]) // 2
    margin = jnp.where((source_of == ranking[0]) | (sink == ranking[0]) | (lengths[sink] == 0), 0, jnp.maximum(margin, 0))
    shifted = jax.random.randint(jax.random.fold_in(own, 4), (amount // 2,), 0, 1 << 20) % (margin + 1)
    lengths = lengths.at[source_of].add(-shifted).at[sink].add(shifted)
    items = jnp.searchsorted(jnp.cumsum(lengths), jnp.arange(rows * top), side="right").astype(jnp.int32)
    listing = items.reshape(top, rows).T
    listing = listing[jax.random.permutation(jax.random.fold_in(own, 1), rows)]
    turn = jax.random.randint(jax.random.fold_in(own, 2), (rows, 1), 0, top)
    return jnp.take_along_axis(listing, (jnp.arange(top)[None, :] + turn) % top, axis=1)


def shares(amount, total, limit, slope, full):
    portions = [(1 << 20) // math.isqrt(standing ** slope) + 1 for standing in range(1, amount + 1)]
    largest = limit if full else min(limit, max(-(-total // amount), total * portions[0] // sum(portions)))
    least = 1 if total - largest >= amount - 1 else 0
    given, spare = [largest] + [least] * (amount - 1), total - largest - least * (amount - 1)
    while spare > 0:
        candidates = [i for i in range(1, amount) if given[i] < largest] or [i for i in range(1, amount) if given[i] < limit]
        pool, remaining = sum([portions[i] for i in candidates]), spare
        for i in candidates:
            extra = min(limit - given[i], max(1, remaining * portions[i] // pool), spare)
            given[i] = given[i] + extra
            spare = spare - extra
    return np.array(given)


def normal_values(key, dims, deviation, bound, pieces=(), held_as=jnp.bfloat16):
    gain = block_scale(key, dims, pieces, -0.22, 0.18) if pieces else 1.0
    values = jax.random.normal(key, dims, jnp.float32) * deviation * gain
    return jnp.minimum(jnp.maximum(values, -bound), bound).astype(held_as)


def setup_inputs(seed: int = 0) -> dict:
    arg_keys = jax.random.split(jax.random.key(seed), 9)
    inverses = draw_inverses(jax.random.fold_in(arg_keys[8], 71), 0)
    table = normal_values(arg_keys[1], (BRICKS, P_SIZE, N), 0.04, 0.23925781, ((0, 16), (2, 16)))
    spots = jnp.clip(1.0 * jax.random.uniform(arg_keys[2], (3, ROUNDS, WALKERS, K), jnp.float32) ** block_scale(arg_keys[2], (3, ROUNDS, WALKERS, K), ((2, 16),), -0.2, 0.2), 0.0, 1.0)
    groups_keys = jax.random.split(jax.random.fold_in(arg_keys[3], 1), ROUNDS * WALKERS * K // K)
    groups_turns = jax.random.permutation(jax.random.fold_in(arg_keys[3], 3), ROUNDS * WALKERS * K // K)
    groups = jax.vmap(lambda own, number: shared_out(jax.random.fold_in(arg_keys[3], 2), own, number, K, WALKERS, 1, CAP, 2))(groups_keys, groups_turns).reshape((ROUNDS, WALKERS, K, 1))
    bricks = with_ends(jax.random.randint(arg_keys[4], (ROUNDS, WALKERS, K), 0, REG_DEV), jax.random.fold_in(arg_keys[4], 1), 0, REG_DEV - 1).astype(jnp.int32)
    accept = with_ends((jax.random.randint(arg_keys[5], (ROUNDS, WALKERS, K), 0, 4) < 3).astype(jnp.int32), jax.random.fold_in(arg_keys[5], 1), 0, 1)
    movers = draw_movers(jax.random.fold_in(arg_keys[8], 71), 0)
    old_rows = normal_values(arg_keys[7], (ROUNDS, WALKERS, K, N), 0.013, 0.079589844, ((1, 16), (3, 16)))
    return {"inverses": inverses, "table": table, "spots": spots, "groups": groups, "bricks": bricks, "accept": accept, "movers": movers, "old_rows": old_rows}


highest = lax.Precision.HIGHEST


def bspline(fraction):
    remain = 1.0 - fraction
    square = fraction * fraction
    cubed = square * fraction
    return jnp.stack([remain * remain * remain / 6.0,
                      (3.0 * cubed - 6.0 * square + 4.0) / 6.0,
                      (-3.0 * cubed + 3.0 * square + 3.0 * fraction + 1.0) / 6.0,
                      cubed / 6.0], axis=-1)


def stencil(spot_rows):
    first = bspline(spot_rows[..., 0])
    second = bspline(spot_rows[..., 1])
    third = bspline(spot_rows[..., 2])
    joined = first[..., :, None, None] * second[..., None, :, None] * third[..., None, None, :]
    return joined.reshape(spot_rows.shape[:-1] + (64,))


def newton(matrix, identity):
    approx = identity
    for repeat in range(NEWTON):
        approx = jnp.dot(approx, 2.0 * identity - jnp.dot(matrix, approx, precision=highest), precision=highest)
    return approx


def reference(inverses, table, spots, groups, bricks, accept, movers, old_rows):
    float_type = inverses.dtype
    positions = jnp.transpose(spots, (2, 1, 3, 0))
    servers = jnp.transpose(groups[..., 0], (1, 0, 2))
    brick_ids = jnp.transpose(bricks, (1, 0, 2))
    accepted = jnp.transpose(accept, (1, 0, 2))
    electrons = jnp.transpose(movers, (1, 0, 2))
    previous = jnp.transpose(old_rows, (1, 0, 2, 3))

    def one_walker(packed):
        inverse, spot_rows, server, brick_row, accepted_row, electron_row, previous_row = packed
        for window in range(ROUNDS):
            brick_rows = (server[window] * REG_DEV + brick_row[window]).astype(jnp.int32)
            weights = stencil(spot_rows[window]).astype(jnp.bfloat16).astype(jnp.float32)
            coeffs = table[brick_rows].astype(jnp.float32)
            values = jnp.einsum('kp,kpn->kn', weights, coeffs).astype(jnp.bfloat16)
            change = accepted_row[window].astype(float_type)[:, None] * (values.astype(float_type) - previous_row[window].astype(float_type))
            product = jnp.dot(change, inverse, precision=highest)
            columns = inverse[:, electron_row[window]]
            ratios = product[:, electron_row[window]]
            identity = jnp.eye(K, dtype=float_type)
            solved = newton(identity + ratios, identity)
            factor = jnp.dot(solved, product, precision=highest)
            inverse = inverse - jnp.dot(columns, factor, precision=highest)
        return inverse

    return lax.map(one_walker, (inverses, positions, servers, brick_ids, accepted, electrons, previous))
```

```python
import jax
import jax.numpy as jnp
from jax import lax
from jax.experimental import pallas as pl
from jax.experimental.pallas import tpu as pltpu
from jax.sharding import PartitionSpec as P

N = 4096
K = 64
ROUNDS = 6
CAP = 8
SERVERS = 16
COLS = 16
BLOCK = N // COLS
ALL = ROUNDS * K
SIDE = 4
SHARE = 48
SLOTS = ROUNDS * CAP
HIGHEST = lax.Precision.HIGHEST
NT = (((1,), (1,)), ((), ()))
bf16 = jnp.bfloat16
f32 = jnp.float32
VMEM = pl.BlockSpec(memory_space=pltpu.VMEM)
ANY = pl.BlockSpec(memory_space=pl.ANY)
SMEM = pl.BlockSpec(memory_space=pltpu.SMEM)


def iota(shape, dim):
    return lax.broadcasted_iota(jnp.int32, shape, dim)


def to_column(row):
    count = row.shape[1]
    square = jnp.broadcast_to(row, (count, count))
    same = iota((count, count), 0) == iota((count, count), 1)
    return jnp.sum(jnp.where(same, square, 0), axis=1, keepdims=True)


def plan_kernel(
    groups_ref, bricks_ref, accept_ref, movers_ref, spots_ref,
    send_ref, target_ref, movers_row_ref, key_ref,
):
    total = jnp.zeros((SERVERS * CAP, 128), f32)
    earlier = iota((K, K), 0) < iota((K, K), 1)
    mover_cols = []
    for window in range(ROUNDS):
        server_row = groups_ref[window]
        server_col = to_column(server_row)
        same = jnp.broadcast_to(server_row, (K, K)) == jnp.broadcast_to(server_col, (K, K))
        order_row = jnp.sum(jnp.where(same & earlier, 1, 0), axis=0, keepdims=True)
        place_row = server_row * CAP + order_row
        placed = jnp.where(
            iota((SERVERS * CAP, K), 0) == jnp.broadcast_to(place_row, (SERVERS * CAP, K)), 1.0, 0.0
        ).astype(f32)
        field = iota((8, K), 0)
        rows = jnp.where(field == 0, spots_ref[0, window], 0.0)
        rows = jnp.where(field == 1, spots_ref[1, window], rows)
        rows = jnp.where(field == 2, spots_ref[2, window], rows)
        rows = jnp.where(field == 3, (bricks_ref[window] + 1).astype(f32), rows)
        parts = []
        if window:
            parts.append(jnp.zeros((8 * window, K), f32))
        parts.append(rows)
        parts.append(jnp.zeros((120 - 8 * window, K), f32))
        total = total + lax.dot_general(
            placed, jnp.concatenate(parts, axis=0), NT, precision=HIGHEST,
            preferred_element_type=f32,
        )
        answer_row = server_row * SLOTS + window * CAP + order_row
        code = to_column(answer_row * 2 + accept_ref[window])
        target_ref[window * K : (window + 1) * K, :] = jnp.broadcast_to(code, (K, 128))
        movers_row_ref[:, window * K : (window + 1) * K] = movers_ref[window]
        mover_cols.append(to_column(movers_ref[window]))
    owner_row = movers_row_ref[...] // BLOCK
    owner_col = jnp.concatenate(mover_cols, axis=0) // BLOCK
    same = jnp.broadcast_to(owner_row, (ALL, ALL)) == jnp.broadcast_to(owner_col, (ALL, ALL))
    before = iota((ALL, ALL), 1) < iota((ALL, ALL), 0)
    rank_col = jnp.sum(jnp.where(same & before, 1, 0), axis=1, keepdims=True)
    key_ref[...] = jnp.broadcast_to(owner_col * ALL + rank_col, (ALL, 128))
    turns = jnp.max(rank_col, axis=0, keepdims=True) // SHARE + 1
    lane = iota((SERVERS * CAP, 128), 1)
    turns = jnp.broadcast_to(turns, (SERVERS * CAP, 128)).astype(f32)
    send_ref[...] = jnp.where(lane == 127, turns, total)


def basis_at(fraction, which):
    remain = 1.0 - fraction
    square = fraction * fraction
    cubed = square * fraction
    first = remain * remain * remain / 6.0
    second = (3.0 * cubed - 6.0 * square + 4.0) / 6.0
    third = (-3.0 * cubed + 3.0 * square + 3.0 * fraction + 1.0) / 6.0
    fourth = cubed / 6.0
    return jnp.where(
        which == 0, first, jnp.where(which == 1, second, jnp.where(which == 2, third, fourth))
    )


def serve_kernel(got_ref, table_ref, out_ref, turns_ref):
    turns_ref[0] = jnp.max(got_ref[:, 127:128]).astype(jnp.int32)
    rows = SERVERS * CAP
    point = iota((rows, 128), 1) % 64
    answers = []
    for window in range(ROUNDS):
        def column(field):
            at = 8 * window + field
            return jnp.broadcast_to(got_ref[:, at : at + 1], (rows, 128))
        weight = (
            basis_at(column(0), point // 16)
            * basis_at(column(1), (point // 4) % 4)
            * basis_at(column(2), point % 4)
        )
        brick = column(3).astype(jnp.int32) - 1
        half = iota((rows, 128), 1) // 64
        spread = jnp.concatenate(
            [jnp.where(brick == 2 * pair + half, weight, 0.0).astype(bf16) for pair in range(16)],
            axis=1,
        )
        answer = jnp.dot(spread, table_ref[...], preferred_element_type=f32)
        answers.append(answer.reshape(SERVERS, CAP, BLOCK))
        if window % 2:
            out_ref[:, (window - 1) * CAP : (window + 1) * CAP, :] = jnp.concatenate(
                answers[-2:], axis=1
            ).astype(bf16)


def collect_kernel(target_ref, answers_ref, old_ref, out_ref):
    code = target_ref[...]
    target = code // 2
    onehot = jnp.concatenate(
        [
            jnp.where(target == piece * 128 + iota((ALL, 128), 1), 1.0, 0.0).astype(bf16)
            for piece in range(SERVERS * SLOTS // 128)
        ],
        axis=1,
    )
    values = jnp.dot(onehot, answers_ref[...], preferred_element_type=f32)
    accepted = jnp.concatenate([code % 2, code % 2], axis=1).astype(f32)
    values = values.astype(bf16).astype(f32)
    out_ref[...] = (accepted * (values - old_ref[...].astype(f32))).astype(bf16)


def pick_kernel(turn_ref, movers_ref, key_ref, inverse_ref, out_ref, chosen):
    @pl.when(pl.program_id(0) == 0)
    def _():
        local_row = movers_ref[...] - lax.axis_index("col") * BLOCK
        placed = jnp.where(
            jnp.broadcast_to(local_row, (BLOCK, ALL)) == iota((BLOCK, ALL), 0), 1.0, 0.0
        ).astype(bf16)
        rank = key_ref[...] % ALL - turn_ref[0] * SHARE
        ranked = jnp.where(rank == iota((ALL, 128), 1), 1.0, 0.0).astype(bf16)
        picks = jnp.dot(placed, ranked, preferred_element_type=f32)
        chosen[...] = picks.T[:SHARE].astype(bf16)

    picked = lax.dot_general(
        chosen[...], inverse_ref[...].astype(bf16), NT, preferred_element_type=f32
    ).astype(bf16)
    for piece in range(out_ref.shape[0]):
        out_ref[piece] = picked[:, piece * BLOCK : (piece + 1) * BLOCK]


def place_kernel(turn_ref, key_ref, got_ref, out_ref):
    key = key_ref[...]
    rank = key % ALL - turn_ref[0] * SHARE
    spot = jnp.where((rank >= 0) & (rank < SHARE), (key // ALL) * SHARE + rank, -1)
    onehot = jnp.concatenate(
        [
            jnp.where(spot == piece * 128 + iota((ALL, 128), 1), 1.0, 0.0).astype(bf16)
            for piece in range(COLS * SHARE // 128)
        ],
        axis=1,
    )
    out_ref[...] = jnp.dot(onehot, got_ref[...], preferred_element_type=f32).T.astype(bf16)


def pick(turn, movers_row, key, inverse):
    step = 4
    return pl.pallas_call(
        pick_kernel,
        grid=(COLS // step,),
        in_specs=[
            SMEM,
            pl.BlockSpec((1, ALL), lambda i: (0, 0)),
            pl.BlockSpec((ALL, 128), lambda i: (0, 0)),
            pl.BlockSpec((step * BLOCK, BLOCK), lambda i: (i, 0)),
        ],
        out_specs=pl.BlockSpec((step, SHARE, BLOCK), lambda i: (i, 0, 0)),
        out_shape=jax.ShapeDtypeStruct((COLS, SHARE, BLOCK), bf16),
        scratch_shapes=[pltpu.VMEM((SHARE, BLOCK), bf16)],
        compiler_params=pltpu.CompilerParams(vmem_limit_bytes=10 * 2**20),
        cost_estimate=pl.CostEstimate(flops=10**8, bytes_accessed=5 * 10**6, transcendentals=0),
        name="pick",
    )(turn, movers_row, key, inverse)


def simple(kernel, shapes, *args, specs=None, outs=None, limit=16 * 2**20, name=None):
    many = isinstance(shapes, (list, tuple))
    return pl.pallas_call(
        kernel,
        in_specs=specs or [VMEM] * len(args),
        out_specs=outs or ([VMEM] * len(shapes) if many else VMEM),
        out_shape=shapes,
        compiler_params=pltpu.CompilerParams(vmem_limit_bytes=limit),
        name=name,
    )(*args)


def shift(rows, columns):
    return [
        (y * SIDE + x, ((y + rows) % SIDE) * SIDE + (x + columns) % SIDE)
        for y in range(SIDE)
        for x in range(SIDE)
    ]


X_UP, X_DOWN, Y_UP, Y_DOWN = shift(0, 1), shift(0, -1), shift(1, 0), shift(-1, 0)


def send(x, pairs):
    return lax.ppermute(x, "col", pairs)


def ring_small(own, up, down):
    half = own.shape[0] // 2
    before = send(own, up)
    after = send(own, down)
    far = [send(before[:half], up), send(after[half:], down)]
    return jnp.stack([own, before, after, jnp.concatenate(far, axis=0)])


def ring_large(own, up, down):
    before = send(own, up)
    after = send(own, down)
    return [own, before, after, send(before[:2], up), send(after[2:], down)]


STEPS = (0, -1, 1, 2)


def where_is(outer, inner):
    if outer < 3:
        return outer, inner
    return 3 + inner // 2, inner % 2


def update_kernel(*refs):
    change_pieces, base_pieces = refs[0:5], refs[5:10]
    inverse, out_ref = refs[10:12]
    result, work, factors, combined, out_sems = refs[12:]
    own = lax.axis_index("col")
    own_y, own_x = own // SIDE, own % SIDE
    half = ALL // 2

    def blocks():
        for y in range(SIDE):
            for x in range(SIDE):
                block = ((own_y + STEPS[y] + SIDE) % SIDE) * SIDE + (
                    own_x + STEPS[x] + SIDE
                ) % SIDE
                rows = pl.ds(pl.multiple_of(block * BLOCK, BLOCK), BLOCK)
                by_row, by_column = where_is(y, x), where_is(x, y)
                yield block, rows, by_row, by_column

    def add(at, product, first):
        if first:
            work[at] = product
        else:
            work[at] = work[at] + product

    lower, upper = slice(0, half), slice(half, ALL)
    left, right = slice(0, ALL), slice(ALL, ALL + BLOCK)
    for number, (block, rows, by_row, by_column) in enumerate(blocks()):
        known = base_pieces[by_column[0]][by_column[1]]
        for part in (lower, upper):
            change = change_pieces[by_row[0]][by_row[1], part, :]
            add((part, left), jnp.dot(change, known, preferred_element_type=f32), number == 0)
    for number, (block, rows, by_row, by_column) in enumerate(blocks()):
        known = inverse[rows, :].astype(bf16)
        for part in (lower, upper):
            change = change_pieces[by_row[0]][by_row[1], part, :]
            add((part, right), jnp.dot(change, known, preferred_element_type=f32), number == 0)
    same = iota((K, K), 0) == iota((K, K), 1)
    identity = jnp.where(same, 1.0, 0.0).astype(f32)

    def split(value):
        high = value.astype(bf16)
        return high, (value - high.astype(f32)).astype(bf16)

    def multiply(one, other):
        def dot(left, right):
            return jnp.dot(left, right, preferred_element_type=f32)

        return dot(one[0], other[0]) + (dot(one[0], other[1]) + dot(one[1], other[0]))

    for window in range(ROUNDS):
        low, high = window * K, (window + 1) * K
        matrix = identity + work[low:high, low:high]
        matrix_parts = split(matrix)
        approx = 2.0 * identity - matrix
        for repeat in range(2):
            parts = split(approx)
            rest = 2.0 * identity - multiply(matrix_parts, parts)
            approx = multiply(parts, split(rest))
        factor = multiply(split(approx), split(work[low:high, :]))
        factors[low:high, :] = factor
        if window < ROUNDS - 1:
            work[high:, :] = work[high:, :] - multiply(
                split(work[high:, low:high]), split(factor)
            )
    for window in reversed(range(ROUNDS)):
        low, high = window * K, (window + 1) * K
        final = factors[low:high, ALL:]
        combined[low:high, :] = final.astype(bf16)
        if window:
            factors[:low, ALL:] = factors[:low, ALL:] - multiply(
                split(factors[:low, low:high]), split(final)
            )
    copies = []
    for number, (block, rows, by_row, by_column) in enumerate(blocks()):
        result[rows, :] = inverse[rows, :] - jnp.dot(
            base_pieces[by_column[0]][by_column[1]], combined[...], preferred_element_type=f32
        )
        copy = pltpu.make_async_copy(result.at[rows], out_ref.at[rows], out_sems.at[number])
        copy.start()
        copies.append(copy)
    for copy in copies:
        copy.wait()


def local(inverses, table, spots, groups, bricks, accept, movers, old_rows):
    inverse = inverses[0]
    sent, target, movers_row, key = simple(
        plan_kernel,
        [
            jax.ShapeDtypeStruct((SERVERS * CAP, 128), f32),
            jax.ShapeDtypeStruct((ALL, 128), jnp.int32),
            jax.ShapeDtypeStruct((1, ALL), jnp.int32),
            jax.ShapeDtypeStruct((ALL, 128), jnp.int32),
        ],
        groups.reshape(ROUNDS, 1, K),
        bricks,
        accept,
        movers,
        spots,
        limit=None,
        name="plan",
    )
    got = lax.all_to_all(
        sent.reshape(SERVERS, CAP, 128), "walker", split_axis=0, concat_axis=0, tiled=True
    ).reshape(SERVERS * CAP, 128)

    def share(turn):
        turn = turn.reshape(1)
        picked = pick(turn, movers_row, key, inverse)
        arrived = lax.all_to_all(picked, "col", split_axis=0, concat_axis=0, tiled=True)
        return simple(
            place_kernel,
            jax.ShapeDtypeStruct((BLOCK, ALL), bf16),
            turn,
            key,
            arrived.reshape(COLS * SHARE, BLOCK),
            specs=[SMEM, VMEM, VMEM],
            name="place",
        )

    answers, turns = simple(
        serve_kernel,
        [
            jax.ShapeDtypeStruct((SERVERS, SLOTS, BLOCK), bf16),
            jax.ShapeDtypeStruct((1,), jnp.int32),
        ],
        got,
        table.reshape(-1, BLOCK),
        outs=[VMEM, SMEM],
        name="serve",
    )
    base = share(jnp.int32(0))
    _, base = lax.while_loop(
        lambda state: state[0] < turns[0],
        lambda state: (state[0] + 1, state[1] + share(state[0])),
        (jnp.int32(1), base),
    )
    near_base = ring_small(base, Y_UP, Y_DOWN)
    answers = lax.all_to_all(answers, "walker", split_axis=0, concat_axis=0, tiled=True)
    change = simple(
        collect_kernel,
        jax.ShapeDtypeStruct((ALL, BLOCK), bf16),
        target,
        answers.reshape(SERVERS * SLOTS, BLOCK),
        old_rows.reshape(ALL, BLOCK),
        name="collect",
    )
    near_change = ring_small(change, X_UP, X_DOWN)
    near_base, near_change = lax.optimization_barrier((near_base, near_change))
    change_pieces = ring_large(near_change, Y_UP, Y_DOWN)
    base_pieces = ring_large(near_base, X_UP, X_DOWN)
    updated = pl.pallas_call(
        update_kernel,
        in_specs=[VMEM] * 11,
        out_specs=ANY,
        out_shape=jax.ShapeDtypeStruct((N, BLOCK), f32),
        scratch_shapes=[
            pltpu.VMEM((N, BLOCK), f32),
            pltpu.VMEM((ALL, ALL + BLOCK), f32),
            pltpu.VMEM((ALL, ALL + BLOCK), f32),
            pltpu.VMEM((ALL, BLOCK), bf16),
            pltpu.SemaphoreType.DMA((COLS,)),
        ],
        compiler_params=pltpu.CompilerParams(vmem_limit_bytes=26 * 2**20),
        name="update",
    )(*change_pieces, *base_pieces, inverse)
    return updated[None]


def solution(mesh):
    return jax.shard_map(
        local,
        mesh=mesh,
        in_specs=(
            P("walker", None, "col"),
            P("walker", None, "col"),
            P(None, None, "walker", None),
            P(None, "walker", None, None),
            P(None, "walker", None),
            P(None, "walker", None),
            P(None, "walker", None),
            P(None, "walker", None, "col"),
        ),
        out_specs=P("walker", None, "col"),
        check_vma=False,
    )
```

```python
import jax
import jax.numpy as jnp
from jax import lax
from jax.experimental import pallas as pl
from jax.experimental.pallas import tpu as pltpu
from jax.sharding import PartitionSpec as P


N = 4096
K = 64
ROUNDS = 6
CAP = 8
SERVERS = 16
COLS = 16
BLOCK = N // COLS
ALL = ROUNDS * K
SIDE = 4
SHARE = 48
SLOTS = ROUNDS * CAP
HIGHEST = lax.Precision.HIGHEST
NT = (((1,), (1,)), ((), ()))
bf16 = jnp.bfloat16
f32 = jnp.float32
VMEM = pl.BlockSpec(memory_space=pltpu.VMEM)
ANY = pl.BlockSpec(memory_space=pl.ANY)
SMEM = pl.BlockSpec(memory_space=pltpu.SMEM)


def iota(shape, dim):
    return lax.broadcasted_iota(jnp.int32, shape, dim)


def to_column(row):
    count = row.shape[1]
    square = jnp.broadcast_to(row, (count, count))
    same = iota((count, count), 0) == iota((count, count), 1)
    return jnp.sum(jnp.where(same, square, 0), axis=1, keepdims=True)


def plan_kernel(
    groups_ref, bricks_ref, accept_ref, movers_ref, spots_ref,
    send_ref, target_ref, movers_row_ref, key_ref,
):
    total = jnp.zeros((SERVERS * CAP, 128), f32)
    earlier = iota((K, K), 0) < iota((K, K), 1)
    mover_cols = []
    for window in range(ROUNDS):
        server_row = groups_ref[window]
        server_col = to_column(server_row)
        same = jnp.broadcast_to(server_row, (K, K)) == jnp.broadcast_to(server_col, (K, K))
        order_row = jnp.sum(jnp.where(same & earlier, 1, 0), axis=0, keepdims=True)
        place_row = server_row * CAP + order_row
        placed = jnp.where(
            iota((SERVERS * CAP, K), 0) == jnp.broadcast_to(place_row, (SERVERS * CAP, K)), 1.0, 0.0
        ).astype(f32)
        field = iota((8, K), 0)
        rows = jnp.where(field == 0, spots_ref[0, window], 0.0)
        rows = jnp.where(field == 1, spots_ref[1, window], rows)
        rows = jnp.where(field == 2, spots_ref[2, window], rows)
        rows = jnp.where(field == 3, (bricks_ref[window] + 1).astype(f32), rows)
        parts = []
        if window:
            parts.append(jnp.zeros((8 * window, K), f32))
        parts.append(rows)
        parts.append(jnp.zeros((120 - 8 * window, K), f32))
        total = total + lax.dot_general(
            placed, jnp.concatenate(parts, axis=0), NT, precision=HIGHEST,
            preferred_element_type=f32,
        )
        answer_row = server_row * SLOTS + window * CAP + order_row
        code = to_column(answer_row * 2 + accept_ref[window])
        target_ref[window * K : (window + 1) * K, :] = jnp.broadcast_to(code, (K, 128))
        movers_row_ref[:, window * K : (window + 1) * K] = movers_ref[window]
        mover_cols.append(to_column(movers_ref[window]))
    owner_row = movers_row_ref[...] // BLOCK
    owner_col = jnp.concatenate(mover_cols, axis=0) // BLOCK
    same = jnp.broadcast_to(owner_row, (ALL, ALL)) == jnp.broadcast_to(owner_col, (ALL, ALL))
    before = iota((ALL, ALL), 1) < iota((ALL, ALL), 0)
    rank_col = jnp.sum(jnp.where(same & before, 1, 0), axis=1, keepdims=True)
    key_ref[...] = jnp.broadcast_to(owner_col * ALL + rank_col, (ALL, 128))
    turns = jnp.max(rank_col, axis=0, keepdims=True) // SHARE + 1
    lane = iota((SERVERS * CAP, 128), 1)
    turns = jnp.broadcast_to(turns, (SERVERS * CAP, 128)).astype(f32)
    send_ref[...] = jnp.where(lane == 127, turns, total)


def basis_at(fraction, which):
    remain = 1.0 - fraction
    square = fraction * fraction
    cubed = square * fraction
    first = remain * remain * remain / 6.0
    second = (3.0 * cubed - 6.0 * square + 4.0) / 6.0
    third = (-3.0 * cubed + 3.0 * square + 3.0 * fraction + 1.0) / 6.0
    fourth = cubed / 6.0
    return jnp.where(
        which == 0, first, jnp.where(which == 1, second, jnp.where(which == 2, third, fourth))
    )


def serve_kernel(got_ref, table_ref, out_ref, turns_ref):
    turns_ref[0] = jnp.max(got_ref[:, 127:128]).astype(jnp.int32)
    rows = SERVERS * CAP
    point = iota((rows, 128), 1) % 64
    answers = []
    for window in range(ROUNDS):
        def column(field):
            at = 8 * window + field
            return jnp.broadcast_to(got_ref[:, at : at + 1], (rows, 128))

        weight = (
            basis_at(column(0), point // 16)
            * basis_at(column(1), (point // 4) % 4)
            * basis_at(column(2), point % 4)
        )
        brick = column(3).astype(jnp.int32) - 1
        half = iota((rows, 128), 1) // 64
        spread = jnp.concatenate(
            [jnp.where(brick == 2 * pair + half, weight, 0.0).astype(bf16) for pair in range(16)],
            axis=1,
        )
        answer = jnp.dot(spread, table_ref[...], preferred_element_type=f32)
        answers.append(answer.reshape(SERVERS, CAP, BLOCK))
        if window % 2:
            out_ref[:, (window - 1) * CAP : (window + 1) * CAP, :] = jnp.concatenate(
                answers[-2:], axis=1
            ).astype(bf16)


def collect_kernel(target_ref, answers_ref, old_ref, out_ref):
    code = target_ref[...]
    target = code // 2
    onehot = jnp.concatenate(
        [
            jnp.where(target == piece * 128 + iota((ALL, 128), 1), 1.0, 0.0).astype(bf16)
            for piece in range(SERVERS * SLOTS // 128)
        ],
        axis=1,
    )
    values = jnp.dot(onehot, answers_ref[...], preferred_element_type=f32)
    accepted = jnp.concatenate([code % 2, code % 2], axis=1).astype(f32)
    values = values.astype(bf16).astype(f32)
    out_ref[...] = (accepted * (values - old_ref[...].astype(f32))).astype(bf16)


def pick_kernel(turn_ref, movers_ref, key_ref, inverse_ref, out_ref, chosen):
    @pl.when(pl.program_id(0) == 0)
    def _():
        local_row = movers_ref[...] - lax.axis_index("col") * BLOCK
        placed = jnp.where(
            jnp.broadcast_to(local_row, (BLOCK, ALL)) == iota((BLOCK, ALL), 0), 1.0, 0.0
        ).astype(bf16)
        rank = key_ref[...] % ALL - turn_ref[0] * SHARE
        ranked = jnp.where(rank == iota((ALL, 128), 1), 1.0, 0.0).astype(bf16)
        picks = jnp.dot(placed, ranked, preferred_element_type=f32)
        chosen[...] = picks.T[:SHARE].astype(bf16)

    picked = lax.dot_general(
        chosen[...], inverse_ref[...].astype(bf16), NT, preferred_element_type=f32
    ).astype(bf16)
    own = lax.axis_index("col")
    for piece in range(SIDE):
        columns = (piece - own % SIDE + SIDE) % SIDE
        rows = (pl.program_id(0) - own // SIDE + SIDE) % SIDE
        out_ref[columns, rows] = picked[:, piece * BLOCK : (piece + 1) * BLOCK]


def place_kernel(turn_ref, key_ref, *refs):
    got_refs, out_ref = refs[:SIDE], refs[SIDE]
    own = lax.axis_index("col")
    key = key_ref[...]
    rank = key % ALL - turn_ref[0] * SHARE
    owner = key // ALL
    rows = (own // SIDE - owner // SIDE + SIDE) % SIDE
    columns = (own % SIDE - owner % SIDE + SIDE) % SIDE
    spot = jnp.where(
        (rank >= 0) & (rank < SHARE), (rows * SIDE + columns) * SHARE + rank, -1
    )
    onehot = jnp.concatenate(
        [
            jnp.where(spot == piece * 128 + iota((ALL, 128), 1), 1.0, 0.0).astype(bf16)
            for piece in range(COLS * SHARE // 128)
        ],
        axis=1,
    )
    out_ref[...] = jnp.dot(
        onehot,
        jnp.concatenate([ref[...] for ref in got_refs], axis=0),
        preferred_element_type=f32,
    ).T.astype(bf16)


def pick(turn, movers_row, key, inverse):
    return pl.pallas_call(
        pick_kernel,
        grid=(SIDE,),
        in_specs=[
            SMEM,
            pl.BlockSpec((1, ALL), lambda i: (0, 0)),
            pl.BlockSpec((ALL, 128), lambda i: (0, 0)),
            pl.BlockSpec((SIDE * BLOCK, BLOCK), lambda i: (i, 0)),
        ],
        out_specs=pl.BlockSpec((SIDE, SIDE, SHARE, BLOCK), lambda i: (0, 0, 0, 0)),
        out_shape=jax.ShapeDtypeStruct((SIDE, SIDE, SHARE, BLOCK), bf16),
        scratch_shapes=[pltpu.VMEM((SHARE, BLOCK), bf16)],
        compiler_params=pltpu.CompilerParams(vmem_limit_bytes=10 * 2**20),
        cost_estimate=pl.CostEstimate(flops=10**8, bytes_accessed=5 * 10**6, transcendentals=0),
        name="pick",
    )(turn, movers_row, key, inverse)


def simple(kernel, shapes, *args, specs=None, outs=None, limit=16 * 2**20):
    many = isinstance(shapes, (list, tuple))
    return pl.pallas_call(
        kernel,
        in_specs=specs or [VMEM] * len(args),
        out_specs=outs or ([VMEM] * len(shapes) if many else VMEM),
        out_shape=shapes,
        compiler_params=pltpu.CompilerParams(vmem_limit_bytes=limit),
    )(*args)


def shift(rows, columns):
    return [
        (y * SIDE + x, ((y + rows) % SIDE) * SIDE + (x + columns) % SIDE)
        for y in range(SIDE)
        for x in range(SIDE)
    ]


X_UP, X_DOWN, Y_UP, Y_DOWN = shift(0, 1), shift(0, -1), shift(1, 0), shift(-1, 0)


def send(x, pairs):
    return lax.ppermute(x, "col", pairs)


def ring_small(own, up, down):
    half = own.shape[0] // 2
    before = send(own, up)
    after = send(own, down)
    far = [send(before[:half], up), send(after[half:], down)]
    return jnp.stack([own, before, after, jnp.concatenate(far, axis=0)])


def ring_large(own, up, down):
    before = send(own, up)
    after = send(own, down)
    return [own, before, after, send(before[:2], up), send(after[2:], down)]


STEPS = (0, -1, 1, 2)


def where_is(outer, inner):
    if outer < 3:
        return outer, inner
    return 3 + inner // 2, inner % 2


def update_kernel(*refs):
    change_pieces, base_pieces = refs[0:5], refs[5:10]
    inverse, out_ref = refs[10:12]
    result, work, factors, combined, out_sems = refs[12:]
    own = lax.axis_index("col")
    own_y, own_x = own // SIDE, own % SIDE
    half = ALL // 2

    def blocks():
        for y in range(SIDE):
            for x in range(SIDE):
                block = ((own_y + STEPS[y] + SIDE) % SIDE) * SIDE + (
                    own_x + STEPS[x] + SIDE
                ) % SIDE
                rows = pl.ds(pl.multiple_of(block * BLOCK, BLOCK), BLOCK)
                by_row, by_column = where_is(y, x), where_is(x, y)
                yield block, rows, by_row, by_column

    def add(at, product, first):
        if first:
            work[at] = product
        else:
            work[at] = work[at] + product

    lower, upper = slice(0, half), slice(half, ALL)
    left, right = slice(0, ALL), slice(ALL, ALL + BLOCK)
    for number, (block, rows, by_row, by_column) in enumerate(blocks()):
        known = base_pieces[by_column[0]][by_column[1]]
        for part in (lower, upper):
            change = change_pieces[by_row[0]][by_row[1], part, :]
            add((part, left), jnp.dot(change, known, preferred_element_type=f32), number == 0)
    for number, (block, rows, by_row, by_column) in enumerate(blocks()):
        known = inverse[rows, :].astype(bf16)
        for part in (lower, upper):
            change = change_pieces[by_row[0]][by_row[1], part, :]
            add((part, right), jnp.dot(change, known, preferred_element_type=f32), number == 0)
    same = iota((K, K), 0) == iota((K, K), 1)
    identity = jnp.where(same, 1.0, 0.0).astype(f32)

    def split(value):
        high = value.astype(bf16)
        return high, (value - high.astype(f32)).astype(bf16)

    def multiply(one, other):
        def dot(left, right):
            return jnp.dot(left, right, preferred_element_type=f32)

        return dot(one[0], other[0]) + (dot(one[0], other[1]) + dot(one[1], other[0]))

    for window in range(ROUNDS):
        low, high = window * K, (window + 1) * K
        matrix = identity + work[low:high, low:high]
        matrix_parts = split(matrix)
        approx = 2.0 * identity - matrix
        for _ in range(2):
            parts = split(approx)
            rest = 2.0 * identity - multiply(matrix_parts, parts)
            approx = multiply(parts, split(rest))
        factor = multiply(split(approx), split(work[low:high, :]))
        factors[low:high, :] = factor
        if window < ROUNDS - 1:
            work[high:, :] = work[high:, :] - multiply(
                split(work[high:, low:high]), split(factor)
            )
    for window in reversed(range(ROUNDS)):
        low, high = window * K, (window + 1) * K
        final = factors[low:high, ALL:]
        combined[low:high, :] = final.astype(bf16)
        if window:
            factors[:low, ALL:] = factors[:low, ALL:] - multiply(
                split(factors[:low, low:high]), split(final)
            )
    copies = []
    for number, (block, rows, by_row, by_column) in enumerate(blocks()):
        result[rows, :] = inverse[rows, :] - jnp.dot(
            base_pieces[by_column[0]][by_column[1]], combined[...], preferred_element_type=f32
        )
        copy = pltpu.make_async_copy(result.at[rows], out_ref.at[rows], out_sems.at[number])
        copy.start()
        copies.append(copy)
    for copy in copies:
        copy.wait()


def local(inverses, table, spots, groups, bricks, accept, movers, old_rows):
    inverse = inverses[0]
    sent, target, movers_row, key = simple(
        plan_kernel,
        [
            jax.ShapeDtypeStruct((SERVERS * CAP, 128), f32),
            jax.ShapeDtypeStruct((ALL, 128), jnp.int32),
            jax.ShapeDtypeStruct((1, ALL), jnp.int32),
            jax.ShapeDtypeStruct((ALL, 128), jnp.int32),
        ],
        groups.reshape(ROUNDS, 1, K),
        bricks,
        accept,
        movers,
        spots,
        limit=None,
    )
    got = lax.all_to_all(
        sent.reshape(SERVERS, CAP, 128), "walker", split_axis=0, concat_axis=0, tiled=True
    ).reshape(SERVERS * CAP, 128)

    def share(turn, after=None):
        turn = turn.reshape(1)
        picked = pick(turn, movers_row, key, inverse)
        if after is not None:
            picked, after = lax.optimization_barrier((picked, after))
        across = [picked[0]]
        for step in range(1, SIDE):
            across.append(send(picked[step], shift(0, step)))
        down = []
        for step in range(SIDE):
            block = jnp.stack([part[step] for part in across])
            if step:
                block = send(block, shift(step, 0))
            down.append(block.reshape(SIDE * SHARE, BLOCK))
        return simple(
            place_kernel,
            jax.ShapeDtypeStruct((BLOCK, ALL), bf16),
            turn,
            key,
            *down,
            specs=[SMEM] + [VMEM] * (1 + SIDE),
        )

    answers, turns = simple(
        serve_kernel,
        [
            jax.ShapeDtypeStruct((SERVERS, SLOTS, BLOCK), bf16),
            jax.ShapeDtypeStruct((1,), jnp.int32),
        ],
        got,
        table.reshape(-1, BLOCK),
        outs=[VMEM, SMEM],
    )
    base = share(jnp.int32(0), answers)
    _, base = lax.while_loop(
        lambda state: state[0] < turns[0],
        lambda state: (state[0] + 1, state[1] + share(state[0])),
        (jnp.int32(1), base),
    )
    answers = lax.all_to_all(answers, "walker", split_axis=0, concat_axis=0, tiled=True)
    change = simple(
        collect_kernel,
        jax.ShapeDtypeStruct((ALL, BLOCK), bf16),
        target,
        answers.reshape(SERVERS * SLOTS, BLOCK),
        old_rows.reshape(ALL, BLOCK),
    )
    base, change = lax.optimization_barrier((base, change))
    near_change = ring_small(change, X_UP, X_DOWN)
    near_base = ring_small(base, Y_UP, Y_DOWN)
    near_base, near_change = lax.optimization_barrier((near_base, near_change))
    change_pieces = ring_large(near_change, Y_UP, Y_DOWN)
    base_pieces = ring_large(near_base, X_UP, X_DOWN)
    updated = pl.pallas_call(
        update_kernel,
        in_specs=[VMEM] * 11,
        out_specs=ANY,
        out_shape=jax.ShapeDtypeStruct((N, BLOCK), f32),
        scratch_shapes=[
            pltpu.VMEM((N, BLOCK), f32),
            pltpu.VMEM((ALL, ALL + BLOCK), f32),
            pltpu.VMEM((ALL, ALL + BLOCK), f32),
            pltpu.VMEM((ALL, BLOCK), bf16),
            pltpu.SemaphoreType.DMA((COLS,)),
        ],
        compiler_params=pltpu.CompilerParams(vmem_limit_bytes=26 * 2**20),
        name="update",
    )(*change_pieces, *base_pieces, inverse)
    return updated[None]


def solution(mesh):
    return jax.shard_map(
        local,
        mesh=mesh,
        in_specs=(
            P("walker", None, "col"),
            P("walker", None, "col"),
            P(None, None, "walker", None),
            P(None, "walker", None, None),
            P(None, "walker", None),
            P(None, "walker", None),
            P(None, "walker", None),
            P(None, "walker", None, "col"),
        ),
        out_specs=P("walker", None, "col"),
        check_vma=False,
    )
```

```python
import jax
import jax.numpy as jnp
from jax import lax
from jax.experimental import pallas as pl
from jax.experimental.pallas import tpu as pltpu
from jax.sharding import PartitionSpec as P


N = 4096
K = 64
ROUNDS = 6
CAP = 8
SERVERS = 16
COLS = 16
BLOCK = N // COLS
ALL = ROUNDS * K
SIDE = 4
SHARE = 48
SLOTS = ROUNDS * CAP
HIGHEST = lax.Precision.HIGHEST
NT = (((1,), (1,)), ((), ()))
bf16 = jnp.bfloat16
f32 = jnp.float32
VMEM = pl.BlockSpec(memory_space=pltpu.VMEM)
ANY = pl.BlockSpec(memory_space=pl.ANY)
SMEM = pl.BlockSpec(memory_space=pltpu.SMEM)


def iota(shape, dim):
    return lax.broadcasted_iota(jnp.int32, shape, dim)


def to_column(row):
    count = row.shape[1]
    square = jnp.broadcast_to(row, (count, count))
    same = iota((count, count), 0) == iota((count, count), 1)
    return jnp.sum(jnp.where(same, square, 0), axis=1, keepdims=True)


def plan_kernel(
    groups_ref, bricks_ref, accept_ref, movers_ref, spots_ref,
    send_ref, target_ref, movers_row_ref, key_ref,
):
    total = jnp.zeros((SERVERS * CAP, 128), f32)
    earlier = iota((K, K), 0) < iota((K, K), 1)
    mover_cols = []
    for window in range(ROUNDS):
        server_row = groups_ref[window]
        server_col = to_column(server_row)
        same = jnp.broadcast_to(server_row, (K, K)) == jnp.broadcast_to(server_col, (K, K))
        order_row = jnp.sum(jnp.where(same & earlier, 1, 0), axis=0, keepdims=True)
        place_row = server_row * CAP + order_row
        placed = jnp.where(
            iota((SERVERS * CAP, K), 0) == jnp.broadcast_to(place_row, (SERVERS * CAP, K)), 1.0, 0.0
        ).astype(f32)
        field = iota((8, K), 0)
        rows = jnp.where(field == 0, spots_ref[0, window], 0.0)
        rows = jnp.where(field == 1, spots_ref[1, window], rows)
        rows = jnp.where(field == 2, spots_ref[2, window], rows)
        rows = jnp.where(field == 3, (bricks_ref[window] + 1).astype(f32), rows)
        parts = []
        if window:
            parts.append(jnp.zeros((8 * window, K), f32))
        parts.append(rows)
        parts.append(jnp.zeros((120 - 8 * window, K), f32))
        total = total + lax.dot_general(
            placed, jnp.concatenate(parts, axis=0), NT, precision=HIGHEST,
            preferred_element_type=f32,
        )
        answer_row = server_row * SLOTS + window * CAP + order_row
        code = to_column(answer_row * 2 + accept_ref[window])
        target_ref[window * K : (window + 1) * K, :] = jnp.broadcast_to(code, (K, 128))
        movers_row_ref[:, window * K : (window + 1) * K] = movers_ref[window]
        mover_cols.append(to_column(movers_ref[window]))
    owner_row = movers_row_ref[...] // BLOCK
    owner_col = jnp.concatenate(mover_cols, axis=0) // BLOCK
    same = jnp.broadcast_to(owner_row, (ALL, ALL)) == jnp.broadcast_to(owner_col, (ALL, ALL))
    before = iota((ALL, ALL), 1) < iota((ALL, ALL), 0)
    rank_col = jnp.sum(jnp.where(same & before, 1, 0), axis=1, keepdims=True)
    key_ref[...] = jnp.broadcast_to(owner_col * ALL + rank_col, (ALL, 128))
    turns = jnp.max(rank_col, axis=0, keepdims=True) // SHARE + 1
    lane = iota((SERVERS * CAP, 128), 1)
    turns = jnp.broadcast_to(turns, (SERVERS * CAP, 128)).astype(f32)
    send_ref[...] = jnp.where(lane == 127, turns, total)


def basis_at(fraction, which):
    remain = 1.0 - fraction
    square = fraction * fraction
    cubed = square * fraction
    first = remain * remain * remain / 6.0
    second = (3.0 * cubed - 6.0 * square + 4.0) / 6.0
    third = (-3.0 * cubed + 3.0 * square + 3.0 * fraction + 1.0) / 6.0
    fourth = cubed / 6.0
    return jnp.where(
        which == 0, first, jnp.where(which == 1, second, jnp.where(which == 2, third, fourth))
    )


def serve_kernel(got_ref, table_ref, out_ref, turns_ref):
    turns_ref[0] = jnp.max(got_ref[:, 127:128]).astype(jnp.int32)
    rows = SERVERS * CAP
    point = iota((rows, 128), 1) % 64
    answers = []
    for window in range(ROUNDS):
        def column(field):
            at = 8 * window + field
            return jnp.broadcast_to(got_ref[:, at : at + 1], (rows, 128))

        weight = (
            basis_at(column(0), point // 16)
            * basis_at(column(1), (point // 4) % 4)
            * basis_at(column(2), point % 4)
        )
        brick = column(3).astype(jnp.int32) - 1
        half = iota((rows, 128), 1) // 64
        spread = jnp.concatenate(
            [jnp.where(brick == 2 * pair + half, weight, 0.0).astype(bf16) for pair in range(16)],
            axis=1,
        )
        answer = jnp.dot(spread, table_ref[...], preferred_element_type=f32)
        answers.append(answer.reshape(SERVERS, CAP, BLOCK))
        if window % 2:
            out_ref[:, (window - 1) * CAP : (window + 1) * CAP, :] = jnp.concatenate(
                answers[-2:], axis=1
            ).astype(bf16)


def collect_kernel(target_ref, answers_ref, old_ref, out_ref):
    code = target_ref[...]
    target = code // 2
    onehot = jnp.concatenate(
        [
            jnp.where(target == piece * 128 + iota((ALL, 128), 1), 1.0, 0.0).astype(bf16)
            for piece in range(SERVERS * SLOTS // 128)
        ],
        axis=1,
    )
    values = jnp.dot(onehot, answers_ref[...], preferred_element_type=f32)
    accepted = jnp.concatenate([code % 2, code % 2], axis=1).astype(f32)
    values = values.astype(bf16).astype(f32)
    out_ref[...] = (accepted * (values - old_ref[...].astype(f32))).astype(bf16)


def pick_kernel(turn_ref, movers_ref, key_ref, inverse_ref, out_ref, chosen):
    @pl.when(pl.program_id(0) == 0)
    def _():
        local_row = movers_ref[...] - lax.axis_index("col") * BLOCK
        placed = jnp.where(
            jnp.broadcast_to(local_row, (BLOCK, ALL)) == iota((BLOCK, ALL), 0), 1.0, 0.0
        ).astype(bf16)
        rank = key_ref[...] % ALL - turn_ref[0] * SHARE
        ranked = jnp.where(rank == iota((ALL, 128), 1), 1.0, 0.0).astype(bf16)
        picks = jnp.dot(placed, ranked, preferred_element_type=f32)
        chosen[...] = picks.T[:SHARE].astype(bf16)

    picked = lax.dot_general(
        chosen[...], inverse_ref[...].astype(bf16), NT, preferred_element_type=f32
    ).astype(bf16)
    own = lax.axis_index("col")
    for piece in range(SIDE):
        columns = (piece - own % SIDE + SIDE) % SIDE
        rows = (pl.program_id(0) - own // SIDE + SIDE) % SIDE
        out_ref[columns, rows] = picked[:, piece * BLOCK : (piece + 1) * BLOCK]


def place_kernel(turn_ref, key_ref, *refs):
    got_refs, out_ref = refs[:SIDE], refs[SIDE]
    own = lax.axis_index("col")
    key = key_ref[...]
    rank = key % ALL - turn_ref[0] * SHARE
    owner = key // ALL
    rows = (own // SIDE - owner // SIDE + SIDE) % SIDE
    columns = (own % SIDE - owner % SIDE + SIDE) % SIDE
    spot = jnp.where(
        (rank >= 0) & (rank < SHARE), (rows * SIDE + columns) * SHARE + rank, -1
    )
    onehot = jnp.concatenate(
        [
            jnp.where(spot == piece * 128 + iota((ALL, 128), 1), 1.0, 0.0).astype(bf16)
            for piece in range(COLS * SHARE // 128)
        ],
        axis=1,
    )
    out_ref[...] = jnp.dot(
        onehot,
        jnp.concatenate([ref[...] for ref in got_refs], axis=0),
        preferred_element_type=f32,
    ).T.astype(bf16)


def pick(turn, movers_row, key, inverse):
    return pl.pallas_call(
        pick_kernel,
        grid=(SIDE,),
        in_specs=[
            SMEM,
            pl.BlockSpec((1, ALL), lambda i: (0, 0)),
            pl.BlockSpec((ALL, 128), lambda i: (0, 0)),
            pl.BlockSpec((SIDE * BLOCK, BLOCK), lambda i: (i, 0)),
        ],
        out_specs=pl.BlockSpec((SIDE, SIDE, SHARE, BLOCK), lambda i: (0, 0, 0, 0)),
        out_shape=jax.ShapeDtypeStruct((SIDE, SIDE, SHARE, BLOCK), bf16),
        scratch_shapes=[pltpu.VMEM((SHARE, BLOCK), bf16)],
        compiler_params=pltpu.CompilerParams(vmem_limit_bytes=10 * 2**20),
        cost_estimate=pl.CostEstimate(flops=10**8, bytes_accessed=5 * 10**6, transcendentals=0),
        name="pick",
    )(turn, movers_row, key, inverse)


def simple(kernel, shapes, *args, specs=None, outs=None, limit=16 * 2**20):
    many = isinstance(shapes, (list, tuple))
    return pl.pallas_call(
        kernel,
        in_specs=specs or [VMEM] * len(args),
        out_specs=outs or ([VMEM] * len(shapes) if many else VMEM),
        out_shape=shapes,
        compiler_params=pltpu.CompilerParams(vmem_limit_bytes=limit),
    )(*args)


def shift(rows, columns):
    return [
        (y * SIDE + x, ((y + rows) % SIDE) * SIDE + (x + columns) % SIDE)
        for y in range(SIDE)
        for x in range(SIDE)
    ]


X_UP, X_DOWN, Y_UP, Y_DOWN = shift(0, 1), shift(0, -1), shift(1, 0), shift(-1, 0)


def send(x, pairs):
    return lax.ppermute(x, "col", pairs)


def ring_small(own, up, down):
    half = own.shape[0] // 2
    before = send(own, up)
    after = send(own, down)
    far = [send(before[:half], up), send(after[half:], down)]
    return jnp.stack([own, before, after, jnp.concatenate(far, axis=0)])


def ring_large(own, up, down):
    before = send(own, up)
    after = send(own, down)
    return [own, before, after, send(before[:2], up), send(after[2:], down)]


STEPS = (0, -1, 1, 2)


def where_is(outer, inner):
    if outer < 3:
        return outer, inner
    return 3 + inner // 2, inner % 2


def update_kernel(*refs):
    change_pieces, base_pieces = refs[0:5], refs[5:10]
    inverse, out_ref = refs[10:12]
    result, work, factors, combined, out_sems = refs[12:]
    own = lax.axis_index("col")
    own_y, own_x = own // SIDE, own % SIDE
    half = ALL // 2

    def blocks():
        for y in range(SIDE):
            for x in range(SIDE):
                block = ((own_y + STEPS[y] + SIDE) % SIDE) * SIDE + (
                    own_x + STEPS[x] + SIDE
                ) % SIDE
                rows = pl.ds(pl.multiple_of(block * BLOCK, BLOCK), BLOCK)
                by_row, by_column = where_is(y, x), where_is(x, y)
                yield block, rows, by_row, by_column

    def add(at, product, first):
        if first:
            work[at] = product
        else:
            work[at] = work[at] + product

    lower, upper = slice(0, half), slice(half, ALL)
    left, right = slice(0, ALL), slice(ALL, ALL + BLOCK)
    for number, (block, rows, by_row, by_column) in enumerate(blocks()):
        known = base_pieces[by_column[0]][by_column[1]]
        for part in (lower, upper):
            change = change_pieces[by_row[0]][by_row[1], part, :]
            add((part, left), jnp.dot(change, known, preferred_element_type=f32), number == 0)
    for number, (block, rows, by_row, by_column) in enumerate(blocks()):
        known = inverse[rows, :].astype(bf16)
        for part in (lower, upper):
            change = change_pieces[by_row[0]][by_row[1], part, :]
            add((part, right), jnp.dot(change, known, preferred_element_type=f32), number == 0)
    same = iota((K, K), 0) == iota((K, K), 1)
    identity = jnp.where(same, 1.0, 0.0).astype(f32)

    def split(value):
        high = value.astype(bf16)
        return high, (value - high.astype(f32)).astype(bf16)

    def multiply(one, other):
        def dot(left, right):
            return jnp.dot(left, right, preferred_element_type=f32)

        return dot(one[0], other[0]) + (dot(one[0], other[1]) + dot(one[1], other[0]))

    for window in range(ROUNDS):
        low, high = window * K, (window + 1) * K
        matrix = identity + work[low:high, low:high]
        matrix_parts = split(matrix)
        approx = 2.0 * identity - matrix
        for _ in range(2):
            parts = split(approx)
            rest = 2.0 * identity - multiply(matrix_parts, parts)
            approx = multiply(parts, split(rest))
        factor = multiply(split(approx), split(work[low:high, :]))
        factors[low:high, :] = factor
        if window < ROUNDS - 1:
            work[high:, :] = work[high:, :] - multiply(
                split(work[high:, low:high]), split(factor)
            )
    for window in reversed(range(ROUNDS)):
        low, high = window * K, (window + 1) * K
        final = factors[low:high, ALL:]
        combined[low:high, :] = final.astype(bf16)
        if window:
            factors[:low, ALL:] = factors[:low, ALL:] - multiply(
                split(factors[:low, low:high]), split(final)
            )
    copies = []
    for number, (block, rows, by_row, by_column) in enumerate(blocks()):
        result[rows, :] = inverse[rows, :] - jnp.dot(
            base_pieces[by_column[0]][by_column[1]], combined[...], preferred_element_type=f32
        )
        copy = pltpu.make_async_copy(result.at[rows], out_ref.at[rows], out_sems.at[number])
        copy.start()
        copies.append(copy)
    for copy in copies:
        copy.wait()


def local(inverses, table, spots, groups, bricks, accept, movers, old_rows):
    inverse = inverses[0]
    sent, target, movers_row, key = simple(
        plan_kernel,
        [
            jax.ShapeDtypeStruct((SERVERS * CAP, 128), f32),
            jax.ShapeDtypeStruct((ALL, 128), jnp.int32),
            jax.ShapeDtypeStruct((1, ALL), jnp.int32),
            jax.ShapeDtypeStruct((ALL, 128), jnp.int32),
        ],
        groups.reshape(ROUNDS, 1, K),
        bricks,
        accept,
        movers,
        spots,
        limit=None,
    )
    got = lax.all_to_all(
        sent.reshape(SERVERS, CAP, 128), "walker", split_axis=0, concat_axis=0, tiled=True
    ).reshape(SERVERS * CAP, 128)

    def share(turn, after=None):
        turn = turn.reshape(1)
        picked = pick(turn, movers_row, key, inverse)
        if after is not None:
            picked, after = lax.optimization_barrier((picked, after))
        across = [picked[0]]
        for step in range(1, SIDE):
            across.append(send(picked[step], shift(0, step)))
        down = []
        for step in range(SIDE):
            block = jnp.stack([part[step] for part in across])
            if step:
                block = send(block, shift(step, 0))
            down.append(block.reshape(SIDE * SHARE, BLOCK))
        return down

    def place(turn, down):
        return simple(
            place_kernel,
            jax.ShapeDtypeStruct((BLOCK, ALL), bf16),
            turn.reshape(1),
            key,
            *down,
            specs=[SMEM] + [VMEM] * (1 + SIDE),
        )

    answers, turns = simple(
        serve_kernel,
        [
            jax.ShapeDtypeStruct((SERVERS, SLOTS, BLOCK), bf16),
            jax.ShapeDtypeStruct((1,), jnp.int32),
        ],
        got,
        table.reshape(-1, BLOCK),
        outs=[VMEM, SMEM],
    )
    shares = share(jnp.int32(0), answers)
    answers = lax.all_to_all(answers, "walker", split_axis=0, concat_axis=0, tiled=True)
    change = simple(
        collect_kernel,
        jax.ShapeDtypeStruct((ALL, BLOCK), bf16),
        target,
        answers.reshape(SERVERS * SLOTS, BLOCK),
        old_rows.reshape(ALL, BLOCK),
    )
    shares, _ = lax.optimization_barrier((shares, change))
    near_change = ring_small(change, X_UP, X_DOWN)
    base = place(jnp.int32(0), shares)
    _, base = lax.while_loop(
        lambda state: state[0] < turns[0],
        lambda state: (state[0] + 1, state[1] + place(state[0], share(state[0]))),
        (jnp.int32(1), base),
    )
    near_base = ring_small(base, Y_UP, Y_DOWN)
    near_base, near_change = lax.optimization_barrier((near_base, near_change))
    change_pieces = ring_large(near_change, Y_UP, Y_DOWN)
    base_pieces = ring_large(near_base, X_UP, X_DOWN)
    updated = pl.pallas_call(
        update_kernel,
        in_specs=[VMEM] * 11,
        out_specs=ANY,
        out_shape=jax.ShapeDtypeStruct((N, BLOCK), f32),
        scratch_shapes=[
            pltpu.VMEM((N, BLOCK), f32),
            pltpu.VMEM((ALL, ALL + BLOCK), f32),
            pltpu.VMEM((ALL, ALL + BLOCK), f32),
            pltpu.VMEM((ALL, BLOCK), bf16),
            pltpu.SemaphoreType.DMA((COLS,)),
        ],
        compiler_params=pltpu.CompilerParams(vmem_limit_bytes=26 * 2**20),
        name="update",
    )(*change_pieces, *base_pieces, inverse)
    return updated[None]


def solution(mesh):
    return jax.shard_map(
        local,
        mesh=mesh,
        in_specs=(
            P("walker", None, "col"),
            P("walker", None, "col"),
            P(None, None, "walker", None),
            P(None, "walker", None, None),
            P(None, "walker", None),
            P(None, "walker", None),
            P(None, "walker", None),
            P(None, "walker", None, "col"),
        ),
        out_specs=P("walker", None, "col"),
        check_vma=False,
    )
```
